32 devices in a mesh: gx: 4 (over y, x), gy: 8 (over z, core).
Axes of the slice: x: 2, y: 2, z: 4, core: 2. Of those that a mesh axis runs over, the one named last changes fastest.
Arguments:
- eigvecs: float32 [24, 512, 1024], P(None, 'gx', 'gy'), may hold values from -40 to 40
- search_dir: float32 [24, 512, 1024], P(None, 'gx', 'gy'), may hold values from -3 to 3
- conduct: float32 [2, 512, 1024], P(None, 'gx', 'gy'), may hold values from 0.1 to 10
- shift: float32 [512, 1024], P('gx', 'gy'), may hold values from 0.01 to 1
- aggregate: int32 [64, 128], P('gx', 'gy'), may hold values from 0 to 127, as said below
- coarse_cols: int32 [32, 3], P(('gx', 'gy')), may hold values from 0 to 31, as said below
- coarse_vals: bfloat16 [32, 3, 128, 128], P(('gx', 'gy')), may hold values from -85 to 300, as said below
Outputs:
- precond: float32 [24, 512, 1024], P(None, 'gx', 'gy')
- gram_a: float32 [72, 72], replicated
- gram_b: float32 [72, 72], replicated
The draws below stay inside these ranges and needn't reach their ends.
Inputs may be any that keep to these rules, and one draw needn't show every extreme that they name: Within one device's tile of blocks, every aggregate id names the same number of blocks. `coarse_cols`: entry 0 of block row d is d itself; the 3 column blocks of a row are distinct. `coarse_vals`: the diagonal of each self block exceeds the sum of magnitudes of the other entries of its row.
All inputs are finite; a program needn't handle non-finite values.
Results may differ from the reference program's by a relative error of at most 0.0003.
Values may be sent and summed in bfloat16 or wider, within the bound.
A program may use at most 128 MiB of HBM per device.

```python
import math
import jax
import jax.numpy as jnp
from jax import lax

K = 24
CX = 128
CY = 128
AGG_DEV = 128
COARSE_NB = 3
COARSE_SWEEPS = 4
SMOOTH_STEPS = 3
NDEV = 32
NX = 512
NY = 1024
NC = 4096
N_GX = 4
N_GY = 8


def draw_eigvecs(key, part):
    rows = jnp.arange(NX, dtype=jnp.float32) / max(NX - 1, 1)
    rising = jnp.exp(jnp.log(3.0) * rows)[None, :, None]
    base = jnp.clip(jax.random.normal(key, (K, NX, NY), jnp.float32), -4.0, 4.0)
    return base * rising


def draw_aggregate(key, part):
    nbx = CX // 8
    nby = CY // 8
    count = nbx * nby
    tiles = N_GX * N_GY
    scores = jax.random.randint(key, (tiles, count), 0, 2 ** 20) * count + jnp.arange(count, dtype=jnp.int32)[None, :]
    order = jnp.argsort(scores, axis=1, stable=True).astype(jnp.int32)
    ids = order % AGG_DEV
    ids = ids.reshape(N_GX, N_GY, nbx, nby).transpose(0, 2, 1, 3)
    return ids.reshape(N_GX * nbx, N_GY * nby).astype(jnp.int32)


def draw_coarse_cols(key, part):
    scores = jax.random.randint(key, (NDEV, NDEV - 1), 0, 2 ** 20) * NDEV + jnp.arange(NDEV - 1, dtype=jnp.int32)[None, :]
    offsets = jnp.argsort(scores, axis=1, stable=True)[:, :COARSE_NB - 1].astype(jnp.int32) + 1
    rows = jnp.arange(NDEV, dtype=jnp.int32)[:, None]
    return jnp.concatenate([rows, (rows + offsets) % NDEV], axis=1).astype(jnp.int32)


def draw_coarse_vals(key, part):
    key_weak = jax.random.fold_in(key, 11)
    key_diag = jax.random.fold_in(key, 12)
    key_cols = jax.random.fold_in(key, 13)
    key_self = jax.random.fold_in(key, 14)
    key_mags = jax.random.fold_in(key, 15)
    shape = (NDEV, COARSE_NB, AGG_DEV, AGG_DEV)
    row_shape = (NDEV, COARSE_NB, AGG_DEV)
    weak = jnp.clip(0.0001 * jax.random.normal(key_weak, shape, jnp.float32), -0.0003, 0.0003)
    mags = jax.random.uniform(key_mags, row_shape, jnp.float32, 0.15, 0.28)
    top = jax.random.uniform(key_diag, (NDEV, AGG_DEV), jnp.float32, 120.0, 299.0)
    rows = jnp.arange(AGG_DEV, dtype=jnp.int32)[None, None, :]
    other_pick = jax.random.randint(key_cols, row_shape, 0, AGG_DEV).astype(jnp.int32)
    self_pick = ((rows + 1 + jax.random.randint(key_self, row_shape, 0, AGG_DEV - 1)) % AGG_DEV).astype(jnp.int32)
    first_row = (jnp.arange(COARSE_NB, dtype=jnp.int32) == 0)[None, :, None]
    picks = jnp.where(first_row, self_pick, other_pick)
    columns = jnp.arange(AGG_DEV, dtype=jnp.int32)[None, None, None, :]
    strong = (picks[..., None] == columns).astype(jnp.float32) * mags[..., None]
    scale_rows = top[:, None, :, None]
    off = (weak - strong) * scale_rows
    eye = jnp.eye(AGG_DEV, dtype=jnp.float32)[None, None]
    first = (jnp.arange(COARSE_NB) == 0).astype(jnp.float32)[None, :, None, None]
    return (off * (1.0 - first * eye) + first * eye * scale_rows).astype(jnp.bfloat16)


def shard_levels(stream_key, shape, shards, smallest, largest):
    loudness, own = 1.0, jax.random.fold_in(stream_key, 6)
    for dim, blocks in shards:
        steps = jnp.exp(jax.random.uniform(jax.random.fold_in(own, dim), (blocks,), jnp.float32, smallest / len(shards), largest / len(shards)))
        loudness = loudness * jnp.repeat(steps, shape[dim] // blocks).reshape([-1 if axis == dim else 1 for axis in range(len(shape))])
    return loudness


def centred(stream_key, shape, deviation, bound, pieces=(), kind=jnp.bfloat16):
    array = jax.random.normal(stream_key, shape, jnp.float32) * deviation
    if len(pieces) > 0:
        array = shard_levels(stream_key, shape, pieces, -0.22, 0.18) * array
    return jnp.clip(array, min=-bound, max=bound).astype(kind)


def setup_inputs(seed: int = 0) -> dict:
    key_of = jax.random.split(jax.random.key(seed), 8)
    return {
        "eigvecs": draw_eigvecs(jax.random.fold_in(key_of[7], 71), 0),
        "search_dir": centred(key_of[1], (K, NX, NY), 0.5, 3.0, ((1, 4), (2, 8)), jnp.float32),
        "conduct": jnp.clip(jnp.exp(math.log(10.0) - 4.6051702 * jax.random.uniform(key_of[2], (2, NX, NY), jnp.float32) ** shard_levels(key_of[2], (2, NX, NY), ((1, 4), (2, 8)), -0.2, 0.2)), 0.1, 10.0),
        "shift": jnp.clip(jnp.exp(math.log(1.0) - 4.6051702 * jax.random.uniform(key_of[3], (NX, NY), jnp.float32) ** shard_levels(key_of[3], (NX, NY), ((0, 4), (1, 8)), -0.2, 0.2)), 0.01, 1.0),
        "aggregate": draw_aggregate(jax.random.fold_in(key_of[7], 71), 0),
        "coarse_cols": draw_coarse_cols(jax.random.fold_in(key_of[7], 71), 0),
        "coarse_vals": draw_coarse_vals(jax.random.fold_in(key_of[7], 71), 0),
    }


cheb_lo = 0.3
cheb_hi = 2.0
damping = 0.6


def chebyshev(start, resid, inverse, operate, steps, update_last):
    theta = (cheb_hi + cheb_lo) / 2.0
    delta = (cheb_hi - cheb_lo) / 2.0
    sigma = theta / delta
    rho = 1.0 / sigma
    direction = inverse * resid / theta
    start = start + direction
    if steps > 1 or update_last:
        resid = resid - operate(direction)
    for step in range(1, steps):
        rho_new = 1.0 / (2.0 * sigma - rho)
        direction = (rho_new * rho) * direction + (2.0 * rho_new / delta) * (inverse * resid)
        start = start + direction
        if step < steps - 1 or update_last:
            resid = resid - operate(direction)
        rho = rho_new
    return start, resid


def inner(left, right):
    flat_l = left.reshape(left.shape[0], -1)
    flat_r = right.reshape(right.shape[0], -1)
    return lax.dot_general(flat_l, flat_r, (((1,), (1,)), ((), ())), precision=lax.Precision.HIGHEST, preferred_element_type=jnp.float32)


def reference(eigvecs, search_dir, conduct, shift, aggregate, coarse_cols, coarse_vals):
    count = eigvecs.shape[0]
    cond_x = conduct[0]
    cond_y = conduct[1]
    prev_x = jnp.pad(cond_x, ((1, 0), (0, 0)))[:-1]
    prev_y = jnp.pad(cond_y, ((0, 0), (1, 0)))[:, :-1]
    diagonal = cond_x + prev_x + cond_y + prev_y + shift
    inverse = 1.0 / diagonal

    def operate(field):
        ext = jnp.pad(field, ((0, 0), (1, 1), (1, 1)))
        return (diagonal * field - cond_x * ext[:, 2:, 1:-1] - prev_x * ext[:, :-2, 1:-1]
                - cond_y * ext[:, 1:-1, 2:] - prev_y * ext[:, 1:-1, :-2])

    image_x = operate(eigvecs)
    image_p = operate(search_dir)
    lam = jnp.sum(eigvecs * image_x, axis=(1, 2)) / jnp.sum(eigvecs * eigvecs, axis=(1, 2))
    resid = image_x - lam[:, None, None] * eigvecs

    smooth, left = chebyshev(jnp.zeros_like(resid), resid, inverse, operate, SMOOTH_STEPS, True)

    nbx_all = NX // 8
    nby_all = NY // 8
    bx = jnp.arange(nbx_all, dtype=jnp.int32)[:, None]
    by = jnp.arange(nby_all, dtype=jnp.int32)[None, :]
    owner = (bx // (CX // 8)) * N_GY + by // (CY // 8)
    unknown = (owner * AGG_DEV + aggregate).reshape(-1).astype(jnp.int32)
    blocks = left.reshape(count, nbx_all, 8, nby_all, 8).sum(axis=(2, 4)).reshape(count, -1)
    coarse_rhs = jax.ops.segment_sum(blocks.T, unknown, num_segments=NC).T

    weights = coarse_vals.astype(jnp.float32)
    ndev = weights.shape[0]
    coarse_diag = jnp.diagonal(weights[:, 0], axis1=1, axis2=2).reshape(-1)
    corr = damping * coarse_rhs / coarse_diag[None, :]
    for sweep in range(COARSE_SWEEPS - 1):
        picks = corr.reshape(count, ndev, AGG_DEV)[:, coarse_cols]
        prod = jnp.einsum("dkab,ndkb->nda", weights, picks, precision=lax.Precision.HIGHEST).reshape(count, -1)
        corr = corr + damping * (coarse_rhs - prod) / coarse_diag[None, :]

    spread = corr[:, unknown].reshape(count, nbx_all, 1, nby_all, 1)
    fine_corr = jnp.broadcast_to(spread, (count, nbx_all, 8, nby_all, 8)).reshape(count, NX, NY)
    smooth = smooth + fine_corr
    left = left - operate(fine_corr)
    precond, unused = chebyshev(smooth, left, inverse, operate, SMOOTH_STEPS, False)
    image_w = operate(precond)

    basis = [eigvecs, precond, search_dir]
    images = [image_x, image_w, image_p]
    gram_a = jnp.concatenate([jnp.concatenate([inner(s, a) for a in images], axis=1) for s in basis], axis=0)
    gram_b = jnp.concatenate([jnp.concatenate([inner(s, t) for t in basis], axis=1) for s in basis], axis=0)
    return precond, gram_a, gram_b
```

```python
import functools

import jax
import jax.numpy as jnp
from jax import lax
from jax.experimental import pallas as pl
from jax.experimental.pallas import tpu as pltpu
from jax.sharding import PartitionSpec as P

H = 8
LANES = 128
VMEM_CAP = 60 * 1024 * 1024

cheb_lo = 0.3
cheb_hi = 2.0
damping = 0.6
theta = (cheb_hi + cheb_lo) / 2.0
delta = (cheb_hi - cheb_lo) / 2.0
sigma = theta / delta
RHO0 = 1.0 / sigma
RHO1 = 1.0 / (2.0 * sigma - RHO0)
RHO2 = 1.0 / (2.0 * sigma - RHO1)

CONTRACT_LAST = (((1,), (1,)), ((), ()))


def params():
    return pltpu.CompilerParams(vmem_limit_bytes=VMEM_CAP)


def lane_ids(shape):
    return lax.broadcasted_iota(jnp.int32, shape, len(shape) - 1)


def split2(value):
    high = value.astype(jnp.bfloat16)
    low = (value - high.astype(jnp.float32)).astype(jnp.bfloat16)
    return high, low


def pack_kernel(x_ref, p_ref, g_ref, top_ref, bot_ref, left_ref, right_ref):
    count, rows, cols = x_ref.shape
    ids = lane_ids((rows + 2 * H, LANES))
    ids_p = lane_ids((rows, LANES))
    acc_l = [jnp.zeros((rows + 2 * H, LANES), jnp.float32) for _ in range(2)]
    acc_r = [jnp.zeros((rows + 2 * H, LANES), jnp.float32) for _ in range(2)]
    for k in range(count + 4):
        mid = x_ref[k] if k < count else g_ref[k - count]
        ext = jnp.concatenate([top_ref[k], mid, bot_ref[k]], axis=0)
        t, o = divmod(k * H, LANES)
        here = (ids >= o) & (ids < o + H)
        acc_l[t] = jnp.where(here, pltpu.roll(ext, o, 1) if o else ext, acc_l[t])
        acc_r[t] = jnp.where(here, pltpu.roll(ext, (o - (cols - H)) % LANES, 1), acc_r[t])
    for k in range(count):
        o = (count + 4) * H - LANES + k
        here = jnp.where(ids_p == o, 1.0, 0.0)
        zero = jnp.zeros((H, LANES), jnp.float32)
        first = pltpu.roll(p_ref[k], o, 1) * here
        last = pltpu.roll(p_ref[k], (o - (cols - 1)) % LANES, 1) * here
        acc_l[1] = acc_l[1] + jnp.concatenate([zero, first, zero], axis=0)
        acc_r[1] = acc_r[1] + jnp.concatenate([zero, last, zero], axis=0)
    for t in range(2):
        left_ref[:, t * LANES:(t + 1) * LANES] = acc_l[t]
        right_ref[:, t * LANES:(t + 1) * LANES] = acc_r[t]


def apply_ext(v, coef):
    rows, lanes = v.shape
    return (
        coef[0] * v
        - coef[1] * pltpu.roll(v, rows - 1, 0)
        - coef[2] * pltpu.roll(v, 1, 0)
        - coef[3] * pltpu.roll(v, lanes - 1, 1)
        - coef[4] * pltpu.roll(v, 1, 1)
    )


def first_kernel(count, x_ref, p_ref, g_ref, top_ref, bot_ref, ptop_ref, pbot_ref, fl_ref, fr_ref,
                 xe_ref, coef_ref, ax_ref, ap_ref, nd_ref, agg_ref, tmp_l, tmp_r):
    k = pl.program_id(0)
    rows = x_ref.shape[1]
    ext_rows = rows + 2 * H
    ids = lane_ids((ext_rows, LANES))

    def side(t, o):
        right = pltpu.roll(fr_ref[:, t * LANES:(t + 1) * LANES], (LANES - o) % LANES, 1)
        left = pltpu.roll(fl_ref[:, t * LANES:(t + 1) * LANES], (LANES - H - o) % LANES, 1)
        return jnp.where(ids < H, right, jnp.where(ids >= LANES - H, left, 0.0))

    def extended(top, mid, bot, edge):
        return jnp.concatenate([jnp.concatenate([top, mid, bot], axis=0), edge], axis=1)

    @pl.when(k == 0)
    def _():
        def coarse_field(n):
            t, o = divmod((count + n) * H, LANES)
            return extended(top_ref[count + n], g_ref[n], bot_ref[count + n], side(t, o))
        cx = coarse_field(0)
        cy = coarse_field(1)
        shift = coarse_field(2)
        agg = coarse_field(3)
        px = pltpu.roll(cx, 1, 0)
        py = pltpu.roll(cy, 1, 1)
        diag = cx + px + cy + py + shift
        inside = shift > 0.0
        coef_ref[0] = diag
        coef_ref[1] = cx
        coef_ref[2] = px
        coef_ref[3] = cy
        coef_ref[4] = py
        coef_ref[5] = jnp.where(inside, 1.0 / jnp.where(inside, diag, 1.0), 0.0)
        for b in range(ext_rows // H):
            agg_ref[b:b + 1, :] = agg[b * H:b * H + 1, :].astype(jnp.int32)

    per = LANES // H
    t = k // per
    o = (k - t * per) * H
    pick = lambda ref: jnp.where(t == 0, ref[:, 0:LANES], ref[:, LANES:2 * LANES])
    right = pltpu.roll(pick(fr_ref), lax.rem(LANES - o, LANES), 1)
    left = pltpu.roll(pick(fl_ref), lax.rem(2 * LANES - H - o, LANES), 1)
    edge = jnp.where(ids < H, right, jnp.where(ids >= LANES - H, left, 0.0))
    x = x_ref[0]
    xe = extended(top_ref[k], x, bot_ref[k], edge)
    xe_ref[0] = xe
    coef = [coef_ref[n] for n in range(5)]
    axe = apply_ext(xe, coef)
    ax = axe[H:H + rows, 0:LANES]
    ax_ref[0] = ax
    num = jnp.sum(jnp.sum(x * ax, axis=0, keepdims=True), axis=1, keepdims=True)
    den = jnp.sum(jnp.sum(x * x, axis=0, keepdims=True), axis=1, keepdims=True)
    ids1 = lane_ids((1, LANES))
    nd_ref[pl.ds(k, 1), :] = jnp.where(ids1 == 0, num, jnp.where(ids1 == 1, den, 0.0))

    p = p_ref[0]
    op = (count + 4) * H - LANES + k
    ids_p = lane_ids((rows, LANES))
    rows_p = lax.broadcasted_iota(jnp.int32, (rows, LANES), 0)
    after_y = pltpu.roll(fr_ref[H:H + rows, LANES:2 * LANES], lax.rem(2 * LANES - 1 - op, LANES), 1)
    before_y = pltpu.roll(fl_ref[H:H + rows, LANES:2 * LANES], LANES - op, 1)
    up = jnp.where(rows_p == rows - 1, pbot_ref[pl.ds(k, 1), :], pltpu.roll(p, rows - 1, 0))
    dn = jnp.where(rows_p == 0, ptop_ref[pl.ds(k, 1), :], pltpu.roll(p, 1, 0))
    rt = jnp.where(ids_p == LANES - 1, after_y, pltpu.roll(p, LANES - 1, 1))
    lf = jnp.where(ids_p == 0, before_y, pltpu.roll(p, 1, 1))
    c = [coef_ref[n, H:H + rows, 0:LANES] for n in range(5)]
    ap_ref[0] = c[0] * p - c[1] * up - c[2] * dn - c[3] * rt - c[4] * lf


def pre_kernel(count, xe_ref, coef_ref, nd_ref, agg_ref, smooth_ref, left_ref, rhs_ref, sums):
    k = pl.program_id(0)
    coef = [coef_ref[n] for n in range(5)]
    inv = coef_ref[5]
    nd = nd_ref[pl.ds(k, 1), :]
    lam = nd[:, 0:1] / nd[:, 1:2]
    xe = xe_ref[0]
    r = apply_ext(xe, coef) - lam * xe
    d = inv * r / theta
    x = d
    r = r - apply_ext(d, coef)
    for rho, rho_new in ((RHO0, RHO1), (RHO1, RHO2)):
        d = rho_new * rho * d + 2.0 * rho_new / delta * (inv * r)
        x = x + d
        r = r - apply_ext(d, coef)
    smooth_ref[0] = x
    left_ref[0] = r
    rows = xe.shape[0] - 2 * H
    sums[k] = jnp.sum(r[H:H + rows, 0:LANES].reshape(rows // H, H, LANES), axis=1)

    @pl.when(k == count - 1)
    def _():
        groups = rhs_ref.shape[1]
        ids = lax.broadcasted_iota(jnp.int32, (groups, LANES), 0)
        total = jnp.zeros((2 * count, groups), jnp.float32)
        for b in range(rows // H):
            part = sums[:, b, :]
            high, low = split2(part)
            hot = jnp.where(ids == agg_ref[b + 1:b + 2, 0:LANES], 1.0, 0.0).astype(jnp.bfloat16)
            total = total + lax.dot_general(jnp.concatenate([high, low], axis=0), hot, CONTRACT_LAST,
                                            preferred_element_type=jnp.float32)
        rhs_ref[...] = total[:count] + total[count:]


def coarse_kernel(me_ref, cols_ref, rhs_ref, vals_ref, out_ref):
    count, groups = out_ref.shape
    me = me_ref[0]
    eye = (lax.broadcasted_iota(jnp.int32, (groups, groups), 0)
           == lax.broadcasted_iota(jnp.int32, (groups, groups), 1))

    def scale(d):
        full = jnp.where(eye, vals_ref[d, 0].astype(jnp.float32), 0.0)
        return damping / jnp.sum(full, axis=0, keepdims=True)

    def columns(d):
        return [d] + [cols_ref[d * 3 + n] for n in range(1, 3)]

    def update(d, own, others, factor):
        total = jnp.zeros((2 * count, groups), jnp.float32)
        for n, e in enumerate([own] + others):
            high, low = split2(e)
            total = total + lax.dot_general(jnp.concatenate([high, low], axis=0), vals_ref[d, n],
                                            CONTRACT_LAST, preferred_element_type=jnp.float32)
        return own + factor * (rhs_ref[d] - total[:count] - total[count:])

    def start(d):
        return rhs_ref[d] * scale(d)

    ring1 = columns(me)
    first = {}
    for i, d in enumerate(ring1):
        first[(i,)] = (d, scale(d))
    second = {}
    for i, d in enumerate(ring1):
        for n in (1, 2):
            if i > 0:
                e = columns(d)[n]
                second[(i, n)] = (e, scale(e))
    c0 = {key: rhs_ref[d] * f for key, (d, f) in list(first.items()) + list(second.items())}
    c1 = {}
    for i in range(3):
        d, f = first[(i,)]
        others = [c0[(1,)], c0[(2,)]] if i == 0 else [c0[(i, 1)], c0[(i, 2)]]
        c1[(i,)] = update(d, c0[(i,)], others, f)
    for key, (d, f) in second.items():
        others = [start(e) for e in columns(d)[1:]]
        c1[key] = update(d, c0[key], others, f)
    c2 = []
    for i in range(3):
        d, f = first[(i,)]
        others = [c1[(1,)], c1[(2,)]] if i == 0 else [c1[(i, 1)], c1[(i, 2)]]
        c2.append(update(d, c1[(i,)], others, f))
    out_ref[...] = update(me, c2[0], c2[1:], first[(0,)][1])


def post_kernel(count, smooth_ref, left_ref, coef_ref, near_ref, agg_ref, x_ref, p_ref, ax_ref, ap_ref,
                out_ref, ga_ref, gb_ref, spread, w_all, aw_all):
    k = pl.program_id(0)
    ext_rows = smooth_ref.shape[1]
    rows = ext_rows - 2 * H
    blocks = ext_rows // H

    @pl.when(k == 0)
    def _():
        ids = lane_ids((count, LANES))
        for b in range(blocks):
            s = 0 if b == 0 else (2 if b == blocks - 1 else 1)
            idx0 = jnp.broadcast_to(agg_ref[b:b + 1, 0:LANES], (count, LANES))
            idx1 = jnp.broadcast_to(agg_ref[b:b + 1, LANES:2 * LANES], (count, LANES))
            spread[b, :, 0:LANES] = jnp.take_along_axis(near_ref[3 * s + 1], idx0, axis=1)
            lf = jnp.take_along_axis(near_ref[3 * s], idx1, axis=1)
            rt = jnp.take_along_axis(near_ref[3 * s + 2], idx1, axis=1)
            spread[b, :, LANES:2 * LANES] = jnp.where(ids < H, rt, jnp.where(ids >= LANES - H, lf, 0.0))

    coef = [coef_ref[n] for n in range(5)]
    inv = coef_ref[5]
    row = spread[:, pl.ds(k, 1), :]
    fine = jnp.broadcast_to(row, (blocks, H, 2 * LANES)).reshape(ext_rows, 2 * LANES)
    x = smooth_ref[0] + fine
    r = left_ref[0] - apply_ext(fine, coef)
    d = inv * r / theta
    x = x + d
    r = r - apply_ext(d, coef)
    d = RHO1 * RHO0 * d + 2.0 * RHO1 / delta * (inv * r)
    x = x + d
    r = r - apply_ext(d, coef)
    d = RHO2 * RHO1 * d + 2.0 * RHO2 / delta * (inv * r)
    x = x + d
    w = x[H:H + rows, 0:LANES]
    out_ref[0] = w
    w_all[k] = w
    aw_all[k] = apply_ext(x, coef)[H:H + rows, 0:LANES]

    @pl.when(k == count - 1)
    def _():
        trial = [x_ref, w_all, p_ref, ax_ref, aw_all, ap_ref]
        size = 3 * count

        def body(b, total):
            at = pl.multiple_of(b * H, H)
            parts = [jnp.swapaxes(ref[:, pl.ds(at, H), :], 0, 1) for ref in trial]
            for i in range(0, H, 2):
                both = jnp.concatenate(
                    [jnp.concatenate([q[i], q[i + 1]], axis=1) for q in parts], axis=0)
                high, low = split2(both)
                lhs = jnp.concatenate([high[:size], low[:size]], axis=0)
                rhs = jnp.concatenate([high, low], axis=0)
                total = total + lax.dot_general(lhs, rhs, CONTRACT_LAST, preferred_element_type=jnp.float32)
            return total

        total = lax.fori_loop(0, rows // H, body, jnp.zeros((2 * size, 4 * size), jnp.float32))
        total = total[:size] + total[size:]
        total = total[:, :2 * size] + total[:, 2 * size:]
        gb_ref[...] = total[:, :size]
        ga_ref[...] = total[:, size:]


def vmem():
    return pl.BlockSpec(memory_space=pltpu.VMEM)


def per_device(eigvecs, search_dir, conduct, shift, aggregate, coarse_cols, coarse_vals):
    f32 = jnp.float32
    count, rows, cols = eigvecs.shape
    groups = coarse_vals.shape[2]
    ngx, ngy = lax.axis_size("gx"), lax.axis_size("gy")
    ndev = ngx * ngy
    ext_rows = rows + 2 * H
    ext_lanes = 2 * LANES
    both = ("gx", "gy")
    me = (lax.axis_index("gx") * ngy + lax.axis_index("gy")).reshape(1)

    def moved(value, dx, dy):
        pairs = [(i * ngy + j, (i + dx) * ngy + j + dy) for i in range(ngx) for j in range(ngy)
                 if 0 <= i + dx < ngx and 0 <= j + dy < ngy]
        return lax.ppermute(value, both, pairs)

    every_vals = lax.all_gather(coarse_vals[0], both, axis=0, tiled=False)
    every_cols = lax.all_gather(coarse_cols[0], both, axis=0, tiled=False).reshape(-1)

    agg_nodes = jnp.repeat(jnp.repeat(aggregate, H, axis=0), H, axis=1).astype(f32)
    grid_in = jnp.concatenate([conduct, shift[None], agg_nodes[None]], axis=0)
    fields = count + 4

    def border(lo, at):
        return jnp.concatenate(
            [eigvecs[:, lo:lo + H], grid_in[:, lo:lo + H],
             search_dir[:, at].reshape(-1, H, cols)], axis=0)

    top = moved(border(rows - H, rows - 1), 1, 0)
    bot = moved(border(0, 0), -1, 0)

    send_l, send_r = pl.pallas_call(
        pack_kernel,
        out_shape=[jax.ShapeDtypeStruct((ext_rows, ext_lanes), f32)] * 2,
        in_specs=[vmem()] * 5,
        out_specs=[vmem()] * 2,
        compiler_params=params(),
        name="pack",
    )(eigvecs, search_dir, grid_in, top, bot)
    from_l = moved(send_r, 0, 1)
    from_r = moved(send_l, 0, -1)

    field = pl.BlockSpec((1, rows, cols), lambda k: (k, 0, 0))
    wide = pl.BlockSpec((1, ext_rows, ext_lanes), lambda k: (k, 0, 0))

    def whole(*shape):
        return pl.BlockSpec(shape, lambda k: (0,) * len(shape))

    blocks = ext_rows // H
    ptop = top[fields:].reshape(count, cols)
    pbot = bot[fields:].reshape(count, cols)
    xe, coef, image_x, image_p, nd, agg_ext = pl.pallas_call(
        functools.partial(first_kernel, count),
        grid=(count,),
        out_shape=[
            jax.ShapeDtypeStruct((count, ext_rows, ext_lanes), f32),
            jax.ShapeDtypeStruct((6, ext_rows, ext_lanes), f32),
            jax.ShapeDtypeStruct((count, rows, cols), f32),
            jax.ShapeDtypeStruct((count, rows, cols), f32),
            jax.ShapeDtypeStruct((count, LANES), f32),
            jax.ShapeDtypeStruct((blocks, ext_lanes), jnp.int32),
        ],
        in_specs=[field, field, whole(*grid_in.shape), whole(*top.shape), whole(*bot.shape),
                  whole(count, cols), whole(count, cols), whole(ext_rows, ext_lanes),
                  whole(ext_rows, ext_lanes)],
        out_specs=[wide, whole(6, ext_rows, ext_lanes), field, field, whole(count, LANES),
                   whole(blocks, ext_lanes)],
        scratch_shapes=[pltpu.VMEM((8, LANES), f32)] * 2,
        compiler_params=params(),
        name="first",
    )(eigvecs, search_dir, grid_in, top, bot, ptop, pbot, from_l, from_r)

    nd = lax.psum(nd, both)

    smooth, left, rhs = pl.pallas_call(
        functools.partial(pre_kernel, count),
        grid=(count,),
        out_shape=[
            jax.ShapeDtypeStruct((count, ext_rows, ext_lanes), f32),
            jax.ShapeDtypeStruct((count, ext_rows, ext_lanes), f32),
            jax.ShapeDtypeStruct((count, groups), f32),
        ],
        in_specs=[wide, whole(6, ext_rows, ext_lanes), whole(count, LANES), whole(blocks, ext_lanes)],
        out_specs=[wide, wide, whole(count, groups)],
        scratch_shapes=[pltpu.VMEM((count, rows // H, LANES), f32)],
        compiler_params=params(),
        name="pre",
    )(xe, coef, nd, agg_ext)

    every_rhs = lax.all_gather(rhs, both, axis=0, tiled=False)
    corr = pl.pallas_call(
        coarse_kernel,
        out_shape=jax.ShapeDtypeStruct((count, groups), f32),
        in_specs=[pl.BlockSpec(memory_space=pltpu.SMEM), pl.BlockSpec(memory_space=pltpu.SMEM), vmem(), vmem()],
        out_specs=vmem(),
        compiler_params=params(),
        name="coarse",
    )(me, every_cols, every_rhs, every_vals)

    near = jnp.stack([corr if dx == 0 and dy == 0 else moved(corr, dx, dy)
                      for dx in (1, 0, -1) for dy in (1, 0, -1)])

    precond, gram_a, gram_b = pl.pallas_call(
        functools.partial(post_kernel, count),
        grid=(count,),
        out_shape=[
            jax.ShapeDtypeStruct((count, rows, cols), f32),
            jax.ShapeDtypeStruct((3 * count, 3 * count), f32),
            jax.ShapeDtypeStruct((3 * count, 3 * count), f32),
        ],
        in_specs=[wide, wide, whole(6, ext_rows, ext_lanes), whole(9, count, groups), whole(blocks, ext_lanes)]
        + [whole(count, rows, cols)] * 4,
        out_specs=[field, whole(3 * count, 3 * count), whole(3 * count, 3 * count)],
        scratch_shapes=[
            pltpu.VMEM((blocks, count, ext_lanes), f32),
            pltpu.VMEM((count, rows, cols), f32),
            pltpu.VMEM((count, rows, cols), f32),
        ],
        compiler_params=params(),
        name="post",
    )(smooth, left, coef, near, agg_ext, eigvecs, search_dir, image_x, image_p)
    gram_a, gram_b = lax.psum((gram_a, gram_b), both)
    return (precond, gram_a, gram_b)


def solution(mesh):
    placed = (
        P(None, "gx", "gy"),
        P(None, "gx", "gy"),
        P(None, "gx", "gy"),
        P("gx", "gy"),
        P("gx", "gy"),
        P(("gx", "gy"), None),
        P(("gx", "gy"), None, None, None),
    )
    return jax.shard_map(
        per_device,
        mesh=mesh,
        in_specs=placed,
        out_specs=(P(None, "gx", "gy"), P(), P()),
        check_vma=False,
    )
```

```python
import functools

import jax
import jax.numpy as jnp
from jax import lax
from jax.experimental import pallas as pl
from jax.experimental.pallas import tpu as pltpu
from jax.sharding import PartitionSpec as P

H = 8
LANES = 128
VMEM_CAP = 60 * 1024 * 1024

cheb_lo = 0.3
cheb_hi = 2.0
damping = 0.6
theta = (cheb_hi + cheb_lo) / 2.0
delta = (cheb_hi - cheb_lo) / 2.0
sigma = theta / delta
RHO0 = 1.0 / sigma
RHO1 = 1.0 / (2.0 * sigma - RHO0)
RHO2 = 1.0 / (2.0 * sigma - RHO1)

CONTRACT_LAST = (((1,), (1,)), ((), ()))


def params():
    return pltpu.CompilerParams(vmem_limit_bytes=VMEM_CAP)


def lane_ids(shape):
    return lax.broadcasted_iota(jnp.int32, shape, len(shape) - 1)


def split2(value):
    high = value.astype(jnp.bfloat16)
    low = (value - high.astype(jnp.float32)).astype(jnp.bfloat16)
    return high, low


def pack_kernel(x_ref, p_ref, g_ref, top_ref, bot_ref, left_ref, right_ref):
    count, rows, cols = x_ref.shape
    ids = lane_ids((rows + 2 * H, LANES))
    ids_p = lane_ids((rows, LANES))
    acc_l = [jnp.zeros((rows + 2 * H, LANES), jnp.float32) for _ in range(2)]
    acc_r = [jnp.zeros((rows + 2 * H, LANES), jnp.float32) for _ in range(2)]
    for k in range(count + 4):
        mid = x_ref[k] if k < count else g_ref[k - count]
        ext = jnp.concatenate([top_ref[k], mid, bot_ref[k]], axis=0)
        t, o = divmod(k * H, LANES)
        here = (ids >= o) & (ids < o + H)
        acc_l[t] = jnp.where(here, pltpu.roll(ext, o, 1) if o else ext, acc_l[t])
        acc_r[t] = jnp.where(here, pltpu.roll(ext, (o - (cols - H)) % LANES, 1), acc_r[t])
    for k in range(count):
        o = (count + 4) * H - LANES + k
        here = jnp.where(ids_p == o, 1.0, 0.0)
        zero = jnp.zeros((H, LANES), jnp.float32)
        first = pltpu.roll(p_ref[k], o, 1) * here
        last = pltpu.roll(p_ref[k], (o - (cols - 1)) % LANES, 1) * here
        acc_l[1] = acc_l[1] + jnp.concatenate([zero, first, zero], axis=0)
        acc_r[1] = acc_r[1] + jnp.concatenate([zero, last, zero], axis=0)
    for t in range(2):
        left_ref[:, t * LANES:(t + 1) * LANES] = acc_l[t]
        right_ref[:, t * LANES:(t + 1) * LANES] = acc_r[t]


def apply_ext(v, coef):
    rows, lanes = v.shape
    return (
        coef[0] * v
        - coef[1] * pltpu.roll(v, rows - 1, 0)
        - coef[2] * pltpu.roll(v, 1, 0)
        - coef[3] * pltpu.roll(v, lanes - 1, 1)
        - coef[4] * pltpu.roll(v, 1, 1)
    )


def first_kernel(count, x_ref, p_ref, g_ref, top_ref, bot_ref, ptop_ref, pbot_ref, fl_ref, fr_ref,
                 xe_ref, coef_ref, ax_ref, ap_ref, nd_ref, agg_ref):
    k = pl.program_id(0)
    rows = x_ref.shape[1]
    ext_rows = rows + 2 * H
    ids = lane_ids((ext_rows, LANES))

    def side(t, o):
        right = pltpu.roll(fr_ref[:, t * LANES:(t + 1) * LANES], (LANES - o) % LANES, 1)
        left = pltpu.roll(fl_ref[:, t * LANES:(t + 1) * LANES], (LANES - H - o) % LANES, 1)
        return jnp.where(ids < H, right, jnp.where(ids >= LANES - H, left, 0.0))

    def extended(top, mid, bot, edge):
        return jnp.concatenate([jnp.concatenate([top, mid, bot], axis=0), edge], axis=1)

    @pl.when(k == 0)
    def _():
        def coarse_field(n):
            t, o = divmod((count + n) * H, LANES)
            return extended(top_ref[count + n], g_ref[n], bot_ref[count + n], side(t, o))
        cx = coarse_field(0)
        cy = coarse_field(1)
        shift = coarse_field(2)
        agg = coarse_field(3)
        px = pltpu.roll(cx, 1, 0)
        py = pltpu.roll(cy, 1, 1)
        diag = cx + px + cy + py + shift
        inside = shift > 0.0
        coef_ref[0] = diag
        coef_ref[1] = cx
        coef_ref[2] = px
        coef_ref[3] = cy
        coef_ref[4] = py
        coef_ref[5] = jnp.where(inside, 1.0 / jnp.where(inside, diag, 1.0), 0.0)
        for b in range(ext_rows // H):
            agg_ref[b:b + 1, :] = agg[b * H:b * H + 1, :].astype(jnp.int32)

    per = LANES // H
    t = k // per
    o = (k - t * per) * H
    pick = lambda ref: jnp.where(t == 0, ref[:, 0:LANES], ref[:, LANES:2 * LANES])
    right = pltpu.roll(pick(fr_ref), lax.rem(LANES - o, LANES), 1)
    left = pltpu.roll(pick(fl_ref), lax.rem(2 * LANES - H - o, LANES), 1)
    edge = jnp.where(ids < H, right, jnp.where(ids >= LANES - H, left, 0.0))
    x = x_ref[0]
    xe = extended(top_ref[k], x, bot_ref[k], edge)
    xe_ref[0] = xe
    coef = [coef_ref[n] for n in range(5)]
    axe = apply_ext(xe, coef)
    ax = axe[H:H + rows, 0:LANES]
    ax_ref[0] = ax
    num = jnp.sum(jnp.sum(x * ax, axis=0, keepdims=True), axis=1, keepdims=True)
    den = jnp.sum(jnp.sum(x * x, axis=0, keepdims=True), axis=1, keepdims=True)
    rows8 = lax.broadcasted_iota(jnp.int32, (H, LANES), 0)
    both = jnp.where(rows8 == 0, num, jnp.where(rows8 == 1, den, 0.0))
    before = jnp.where(k == 0, 0.0, nd_ref[...])
    nd_ref[...] = jnp.where(lane_ids((H, LANES)) == k, both, before)

    p = p_ref[0]
    op = (count + 4) * H - LANES + k
    ids_p = lane_ids((rows, LANES))
    rows_p = lax.broadcasted_iota(jnp.int32, (rows, LANES), 0)
    after_y = pltpu.roll(fr_ref[H:H + rows, LANES:2 * LANES], lax.rem(2 * LANES - 1 - op, LANES), 1)
    before_y = pltpu.roll(fl_ref[H:H + rows, LANES:2 * LANES], LANES - op, 1)
    up = jnp.where(rows_p == rows - 1, pbot_ref[pl.ds(k, 1), :], pltpu.roll(p, rows - 1, 0))
    dn = jnp.where(rows_p == 0, ptop_ref[pl.ds(k, 1), :], pltpu.roll(p, 1, 0))
    rt = jnp.where(ids_p == LANES - 1, after_y, pltpu.roll(p, LANES - 1, 1))
    lf = jnp.where(ids_p == 0, before_y, pltpu.roll(p, 1, 1))
    c = [coef_ref[n, H:H + rows, 0:LANES] for n in range(5)]
    ap_ref[0] = c[0] * p - c[1] * up - c[2] * dn - c[3] * rt - c[4] * lf


def pre_kernel(count, xe_ref, coef_ref, nd_ref, agg_ref, smooth_ref, left_ref, rhs_ref, sums):
    k = pl.program_id(0)
    coef = [coef_ref[n] for n in range(5)]
    inv = coef_ref[5]
    nd = jnp.sum(jnp.where(lane_ids((H, LANES)) == k, nd_ref[...], 0.0), axis=1, keepdims=True)
    lam = nd[0:1] / nd[1:2]
    xe = xe_ref[0]
    r = apply_ext(xe, coef) - lam * xe
    d = inv * r / theta
    x = d
    r = r - apply_ext(d, coef)
    for rho, rho_new in ((RHO0, RHO1), (RHO1, RHO2)):
        d = rho_new * rho * d + 2.0 * rho_new / delta * (inv * r)
        x = x + d
        r = r - apply_ext(d, coef)
    smooth_ref[0] = x
    left_ref[0] = r
    rows = xe.shape[0] - 2 * H
    sums[k] = jnp.sum(r[H:H + rows, 0:LANES].reshape(rows // H, H, LANES), axis=1)

    @pl.when(k == count - 1)
    def _():
        groups = rhs_ref.shape[1]
        ids = lax.broadcasted_iota(jnp.int32, (groups, LANES), 0)
        total = jnp.zeros((2 * count, groups), jnp.float32)
        for b in range(rows // H):
            part = sums[:, b, :]
            high, low = split2(part)
            hot = jnp.where(ids == agg_ref[b + 1:b + 2, 0:LANES], 1.0, 0.0).astype(jnp.bfloat16)
            total = total + lax.dot_general(jnp.concatenate([high, low], axis=0), hot, CONTRACT_LAST,
                                            preferred_element_type=jnp.float32)
        rhs_ref[...] = total[:count] + total[count:]


def coarse_kernel(me_ref, cols_ref, rhs_ref, vals_ref, out_ref):
    count, groups = out_ref.shape
    me = me_ref[0]
    eye = (lax.broadcasted_iota(jnp.int32, (groups, groups), 0)
           == lax.broadcasted_iota(jnp.int32, (groups, groups), 1))

    def scale(d):
        full = jnp.where(eye, vals_ref[d, 0:groups].astype(jnp.float32), 0.0)
        return damping / jnp.sum(full, axis=0, keepdims=True)

    def columns(d):
        return [d] + [cols_ref[d * 3 + n] for n in range(1, 3)]

    def update(d, own, others, factor):
        total = jnp.zeros((2 * count, groups), jnp.float32)
        for n, e in enumerate([own] + others):
            high, low = split2(e)
            total = total + lax.dot_general(jnp.concatenate([high, low], axis=0), vals_ref[d, n * groups:(n + 1) * groups],
                                            CONTRACT_LAST, preferred_element_type=jnp.float32)
        return own + factor * (rhs_ref[d] - total[:count] - total[count:])

    def start(d):
        return rhs_ref[d] * scale(d)

    ring1 = columns(me)
    first = {}
    for i, d in enumerate(ring1):
        first[(i,)] = (d, scale(d))
    second = {}
    for i, d in enumerate(ring1):
        for n in (1, 2):
            if i > 0:
                e = columns(d)[n]
                second[(i, n)] = (e, scale(e))
    c0 = {key: rhs_ref[d] * f for key, (d, f) in list(first.items()) + list(second.items())}
    c1 = {}
    for i in range(3):
        d, f = first[(i,)]
        others = [c0[(1,)], c0[(2,)]] if i == 0 else [c0[(i, 1)], c0[(i, 2)]]
        c1[(i,)] = update(d, c0[(i,)], others, f)
    for key, (d, f) in second.items():
        others = [start(e) for e in columns(d)[1:]]
        c1[key] = update(d, c0[key], others, f)
    c2 = []
    for i in range(3):
        d, f = first[(i,)]
        others = [c1[(1,)], c1[(2,)]] if i == 0 else [c1[(i, 1)], c1[(i, 2)]]
        c2.append(update(d, c1[(i,)], others, f))
    out_ref[...] = update(me, c2[0], c2[1:], first[(0,)][1])


def post_kernel(count, smooth_ref, left_ref, coef_ref, near_ref, agg_ref, x_ref, p_ref, ax_ref, ap_ref,
                out_ref, gram_ref, spread, w_all, aw_all):
    k = pl.program_id(0)
    ext_rows = smooth_ref.shape[1]
    rows = ext_rows - 2 * H
    blocks = ext_rows // H

    @pl.when(k == 0)
    def _():
        ids = lane_ids((count, LANES))
        for b in range(blocks):
            s = 0 if b == 0 else (2 if b == blocks - 1 else 1)
            idx0 = jnp.broadcast_to(agg_ref[b:b + 1, 0:LANES], (count, LANES))
            idx1 = jnp.broadcast_to(agg_ref[b:b + 1, LANES:2 * LANES], (count, LANES))
            inside = coef_ref[5, b * H:b * H + 1, :] > 0.0
            own = jnp.take_along_axis(near_ref[3 * s + 1], idx0, axis=1)
            spread[b, :, 0:LANES] = jnp.where(inside[:, 0:LANES], own, 0.0)
            lf = jnp.take_along_axis(near_ref[3 * s], idx1, axis=1)
            rt = jnp.take_along_axis(near_ref[3 * s + 2], idx1, axis=1)
            edge = jnp.where(ids < H, rt, jnp.where(ids >= LANES - H, lf, 0.0))
            spread[b, :, LANES:2 * LANES] = jnp.where(inside[:, LANES:2 * LANES], edge, 0.0)

    coef = [coef_ref[n] for n in range(5)]
    inv = coef_ref[5]
    row = spread[:, pl.ds(k, 1), :]
    fine = jnp.broadcast_to(row, (blocks, H, 2 * LANES)).reshape(ext_rows, 2 * LANES)
    x = smooth_ref[0] + fine
    r = left_ref[0] - apply_ext(fine, coef)
    d = inv * r / theta
    x = x + d
    r = r - apply_ext(d, coef)
    d = RHO1 * RHO0 * d + 2.0 * RHO1 / delta * (inv * r)
    x = x + d
    r = r - apply_ext(d, coef)
    d = RHO2 * RHO1 * d + 2.0 * RHO2 / delta * (inv * r)
    x = x + d
    w = x[H:H + rows, 0:LANES]
    out_ref[0] = w
    w_all[k] = w
    aw_all[k] = apply_ext(x, coef)[H:H + rows, 0:LANES]

    @pl.when(k == count - 1)
    def _():
        trial = [x_ref, w_all, p_ref, aw_all, ap_ref, ax_ref]
        size = 3 * count

        def body(b, total):
            at = pl.multiple_of(b * H, H)
            parts = [jnp.swapaxes(ref[:, pl.ds(at, H), :], 0, 1) for ref in trial]
            for i in range(0, H, 2):
                both = jnp.concatenate(
                    [jnp.concatenate([q[i], q[i + 1]], axis=1) for q in parts], axis=0)
                high, low = split2(both)
                lhs = jnp.concatenate([high[:size], low[:size]], axis=0)
                rhs = jnp.concatenate([high, low], axis=0)
                total = total + lax.dot_general(lhs, rhs, CONTRACT_LAST, preferred_element_type=jnp.float32)
            return total

        total = lax.fori_loop(0, rows // H, body, jnp.zeros((2 * size, 4 * size), jnp.float32))
        total = total[:size] + total[size:]
        total = total[:, :2 * size] + total[:, 2 * size:]
        gram_ref[0:size, :] = total[:, 0:LANES]
        rest = total[0:count, LANES:2 * size]
        pad = jnp.zeros((count, 2 * LANES - 2 * size), jnp.float32)
        gram_ref[size:size + count, :] = jnp.concatenate([rest, pad], axis=1)


def vmem():
    return pl.BlockSpec(memory_space=pltpu.VMEM)


def greet(peers):
    barrier = pltpu.get_barrier_semaphore()
    for peer in peers:
        pl.semaphore_signal(barrier, inc=1, device_id=peer, device_id_type=pl.DeviceIdType.MESH)
    pl.semaphore_wait(barrier, len(peers))


def sent(src, dst, send, recv, peer):
    copy = pltpu.make_async_remote_copy(src_ref=src, dst_ref=dst, send_sem=send, recv_sem=recv,
                                        device_id=peer, device_id_type=pl.DeviceIdType.MESH)
    copy.start()
    return copy


def summed(slots, number):
    total = slots[0]
    for n in range(1, number):
        total = total + slots[n]
    return total


def total_kernel(ngx, ngy, in_ref, out_ref, slots1, slots2, send1, recv1, send2, recv2):
    i, j = lax.axis_index("gx"), lax.axis_index("gy")
    peers_y = [(i, lax.rem(j + o, ngy)) for o in range(1, ngy)]
    peers_x = [(lax.rem(i + o, ngx), j) for o in range(1, ngx)]
    greet(peers_y + peers_x)
    copies = [sent(in_ref, slots1.at[j], send1.at[n], recv1.at[n], p) for n, p in enumerate(peers_y)]
    slots1[j] = in_ref[...]
    for copy in copies:
        copy.wait()
    slots2[i] = summed(slots1, ngy)
    copies = [sent(slots2.at[i], slots2.at[i], send2.at[n], recv2.at[n], p) for n, p in enumerate(peers_x)]
    for copy in copies:
        copy.wait()
    out_ref[...] = summed(slots2, ngx)


def halves_total_kernel(ngx, ngy, in_ref, out_ref, slots1, slots2, send1, recv1, send2, recv2,
                        part, pair, send0, recv0):
    i, j = lax.axis_index("gx"), lax.axis_index("gy")
    nz, half = ngy // 2, in_ref.shape[0] // 2
    z, c = j // 2, lax.rem(j, 2)
    partner = (i, j + 1 - 2 * c)
    peers_z = [(i, lax.rem(z + o, nz) * 2 + c) for o in range(1, nz)]
    peers_x = [(lax.rem(i + o, ngx), j) for o in range(1, ngx)]
    greet([partner] + peers_z + peers_x)
    mine = pl.ds(pl.multiple_of(c * half, half), half)
    theirs = pl.ds(pl.multiple_of((1 - c) * half, half), half)
    sent(in_ref.at[theirs], part, send0.at[0], recv0.at[0], partner).wait()
    slots1[z] = in_ref[mine] + part[...]
    copies = [sent(slots1.at[z], slots1.at[z], send1.at[n], recv1.at[n], p) for n, p in enumerate(peers_z)]
    for copy in copies:
        copy.wait()
    slots2[i] = summed(slots1, nz)
    copies = [sent(slots2.at[i], slots2.at[i], send2.at[n], recv2.at[n], p) for n, p in enumerate(peers_x)]
    for copy in copies:
        copy.wait()
    pair[c] = summed(slots2, ngx)
    sent(pair.at[c], pair.at[c], send0.at[1], recv0.at[1], partner).wait()
    out_ref[0:half] = pair[0]
    out_ref[half:2 * half] = pair[1]


def remote_params(number):
    return pltpu.CompilerParams(vmem_limit_bytes=VMEM_CAP, collective_id=number, has_side_effects=True)


def total_call(kernel, value, ngx, ngy, number):
    rows, lanes = value.shape
    halves = number == 1
    first, rows1 = (ngy // 2, rows // 2) if halves else (ngy, rows)
    dma = pltpu.SemaphoreType.DMA
    scratch = [pltpu.VMEM((first, rows1, lanes), jnp.float32), pltpu.VMEM((ngx, rows1, lanes), jnp.float32),
               dma((first - 1,)), dma((first - 1,)), dma((ngx - 1,)), dma((ngx - 1,))]
    if halves:
        scratch += [pltpu.VMEM((rows1, lanes), jnp.float32), pltpu.VMEM((2, rows1, lanes), jnp.float32),
                    dma((2,)), dma((2,))]
    return pl.pallas_call(
        kernel, out_shape=jax.ShapeDtypeStruct(value.shape, value.dtype),
        in_specs=[vmem()], out_specs=vmem(), scratch_shapes=scratch,
        compiler_params=remote_params(number), name="total",
    )(value)


def gather_kernel(ngx, ngy, in_ref, out_ref, send1, recv1, send2, recv2, local):
    i, j = lax.axis_index("gx"), lax.axis_index("gy")
    peers_y = [(i, lax.rem(j + o, ngy)) for o in range(1, ngy)]
    peers_x = [(lax.rem(i + o, ngx), j) for o in range(1, ngx)]
    me = i * ngy + j
    own = pltpu.make_async_copy(in_ref, out_ref.at[me], local)
    own.start()
    greet(peers_y + peers_x)
    copies = [sent(in_ref, out_ref.at[me], send1.at[n], recv1.at[n], p) for n, p in enumerate(peers_y)]
    own.wait()
    for copy in copies:
        copy.wait()
    line = out_ref.at[pl.ds(i * ngy, ngy)]
    copies = [sent(line, line, send2.at[n], recv2.at[n], p) for n, p in enumerate(peers_x)]
    for copy in copies:
        copy.wait()


def gather_call(value, ngx, ngy, number):
    dma = pltpu.SemaphoreType.DMA
    return pl.pallas_call(
        functools.partial(gather_kernel, ngx, ngy),
        out_shape=jax.ShapeDtypeStruct((ngx * ngy,) + value.shape, value.dtype),
        in_specs=[vmem()], out_specs=vmem(),
        scratch_shapes=[dma((ngy - 1,)), dma((ngy - 1,)), dma((ngx - 1,)), dma((ngx - 1,)), dma],
        compiler_params=remote_params(number), name="gather",
    )(value)


def near_kernel(ngx, ngy, in_ref, out_ref, send, recv, local):
    i, j = lax.axis_index("gx"), lax.axis_index("gy")
    steps = [(s, t) for s in range(3) for t in range(3) if (s, t) != (1, 1)]
    peers = [(lax.rem(i + 1 - s + ngx, ngx), lax.rem(j + 1 - t + ngy, ngy)) for s, t in steps]
    own = pltpu.make_async_copy(in_ref, out_ref.at[4], local)
    own.start()
    greet(peers)
    copies = [sent(in_ref, out_ref.at[3 * s + t], send.at[n], recv.at[n], p)
              for n, ((s, t), p) in enumerate(zip(steps, peers))]
    own.wait()
    for copy in copies:
        copy.wait()


def near_call(value, ngx, ngy, number):
    dma = pltpu.SemaphoreType.DMA
    return pl.pallas_call(
        functools.partial(near_kernel, ngx, ngy),
        out_shape=jax.ShapeDtypeStruct((9,) + value.shape, value.dtype),
        in_specs=[vmem()], out_specs=vmem(),
        scratch_shapes=[dma((8,)), dma((8,)), dma],
        compiler_params=remote_params(number), name="near",
    )(value)


def per_device(eigvecs, search_dir, conduct, shift, aggregate, coarse_cols, coarse_vals):
    f32 = jnp.float32
    count, rows, cols = eigvecs.shape
    groups = coarse_vals.shape[2]
    ngx, ngy = lax.axis_size("gx"), lax.axis_size("gy")
    ndev = ngx * ngy
    ext_rows = rows + 2 * H
    ext_lanes = 2 * LANES
    both = ("gx", "gy")
    me = (lax.axis_index("gx") * ngy + lax.axis_index("gy")).reshape(1)

    def moved(value, dx, dy):
        pairs = [(i * ngy + j, (i + dx) * ngy + j + dy) for i in range(ngx) for j in range(ngy)
                 if 0 <= i + dx < ngx and 0 <= j + dy < ngy]
        return lax.ppermute(value, both, pairs)

    listed = jnp.pad(coarse_cols.astype(jnp.bfloat16), ((0, 15), (0, groups - 3)))
    carried = jnp.concatenate([coarse_vals[0].reshape(3 * groups, groups), listed], axis=0)
    every_vals = lax.all_gather(carried, both, axis=0, tiled=False)
    every_cols = every_vals[:, 3 * groups, :3].astype(jnp.int32).reshape(-1)

    agg_nodes = jnp.repeat(jnp.repeat(aggregate, H, axis=0), H, axis=1).astype(f32)
    grid_in = jnp.concatenate([conduct, shift[None], agg_nodes[None]], axis=0)
    fields = count + 4

    def border(lo, at):
        return jnp.concatenate(
            [eigvecs[:, lo:lo + H], grid_in[:, lo:lo + H],
             search_dir[:, at].reshape(-1, H, cols)], axis=0)

    top = moved(border(rows - H, rows - 1), 1, 0)
    bot = moved(border(0, 0), -1, 0)

    send_l, send_r = pl.pallas_call(
        pack_kernel,
        out_shape=[jax.ShapeDtypeStruct((ext_rows, ext_lanes), f32)] * 2,
        in_specs=[vmem()] * 5,
        out_specs=[vmem()] * 2,
        compiler_params=params(),
        name="pack",
    )(eigvecs, search_dir, grid_in, top, bot)
    from_l = moved(send_r, 0, 1)
    from_r = moved(send_l, 0, -1)

    field = pl.BlockSpec((1, rows, cols), lambda k: (k, 0, 0))
    wide = pl.BlockSpec((1, ext_rows, ext_lanes), lambda k: (k, 0, 0))

    def whole(*shape):
        return pl.BlockSpec(shape, lambda k: (0,) * len(shape))

    blocks = ext_rows // H
    ptop = top[fields:].reshape(count, cols)
    pbot = bot[fields:].reshape(count, cols)
    xe, coef, image_x, image_p, nd, agg_ext = pl.pallas_call(
        functools.partial(first_kernel, count),
        grid=(count,),
        out_shape=[
            jax.ShapeDtypeStruct((count, ext_rows, ext_lanes), f32),
            jax.ShapeDtypeStruct((6, ext_rows, ext_lanes), f32),
            jax.ShapeDtypeStruct((count, rows, cols), f32),
            jax.ShapeDtypeStruct((count, rows, cols), f32),
            jax.ShapeDtypeStruct((H, LANES), f32),
            jax.ShapeDtypeStruct((blocks, ext_lanes), jnp.int32),
        ],
        in_specs=[field, field, whole(*grid_in.shape), whole(*top.shape), whole(*bot.shape),
                  whole(count, cols), whole(count, cols), whole(ext_rows, ext_lanes),
                  whole(ext_rows, ext_lanes)],
        out_specs=[wide, whole(6, ext_rows, ext_lanes), field, field, whole(H, LANES),
                   whole(blocks, ext_lanes)],
        compiler_params=params(),
        name="first",
    )(eigvecs, search_dir, grid_in, top, bot, ptop, pbot, from_l, from_r)

    nd = total_call(functools.partial(total_kernel, ngx, ngy), nd, ngx, ngy, 0)

    smooth, left, rhs = pl.pallas_call(
        functools.partial(pre_kernel, count),
        grid=(count,),
        out_shape=[
            jax.ShapeDtypeStruct((count, ext_rows, ext_lanes), f32),
            jax.ShapeDtypeStruct((count, ext_rows, ext_lanes), f32),
            jax.ShapeDtypeStruct((count, groups), f32),
        ],
        in_specs=[wide, whole(6, ext_rows, ext_lanes), whole(H, LANES), whole(blocks, ext_lanes)],
        out_specs=[wide, wide, whole(count, groups)],
        scratch_shapes=[pltpu.VMEM((count, rows // H, LANES), f32)],
        compiler_params=params(),
        name="pre",
    )(xe, coef, nd, agg_ext)

    every_rhs = gather_call(rhs, ngx, ngy, 2)
    corr = pl.pallas_call(
        coarse_kernel,
        out_shape=jax.ShapeDtypeStruct((count, groups), f32),
        in_specs=[pl.BlockSpec(memory_space=pltpu.SMEM), pl.BlockSpec(memory_space=pltpu.SMEM), vmem(), vmem()],
        out_specs=vmem(),
        compiler_params=params(),
        name="coarse",
    )(me, every_cols, every_rhs, every_vals)

    near = near_call(corr, ngx, ngy, 3)

    precond, gram = pl.pallas_call(
        functools.partial(post_kernel, count),
        grid=(count,),
        out_shape=[
            jax.ShapeDtypeStruct((count, rows, cols), f32),
            jax.ShapeDtypeStruct((4 * count, LANES), f32),
        ],
        in_specs=[wide, wide, whole(6, ext_rows, ext_lanes), whole(9, count, groups), whole(blocks, ext_lanes)]
        + [whole(count, rows, cols)] * 4,
        out_specs=[field, whole(4 * count, LANES)],
        scratch_shapes=[
            pltpu.VMEM((blocks, count, ext_lanes), f32),
            pltpu.VMEM((count, rows, cols), f32),
            pltpu.VMEM((count, rows, cols), f32),
        ],
        compiler_params=params(),
        name="post",
    )(smooth, left, coef, near, agg_ext, eigvecs, search_dir, image_x, image_p)
    gram = total_call(functools.partial(halves_total_kernel, ngx, ngy), gram, ngx, ngy, 1)
    c, size = count, 3 * count
    gram_b = gram[:size, :size]
    xaw, xap = gram[:c, size:size + c], gram[:c, size + c:size + 2 * c]
    xax = jnp.concatenate([gram[:c, size + 2 * c:], gram[size:, :2 * size - LANES]], axis=1)
    gram_a = jnp.concatenate([
        jnp.concatenate([xax, xaw, xap], axis=1),
        jnp.concatenate([jnp.concatenate([xaw.T, xap.T], axis=0), gram[c:size, size:size + 2 * c]], axis=1),
    ], axis=0)
    return (precond, gram_a, gram_b)


def solution(mesh):
    placed = (
        P(None, "gx", "gy"),
        P(None, "gx", "gy"),
        P(None, "gx", "gy"),
        P("gx", "gy"),
        P("gx", "gy"),
        P(("gx", "gy"), None),
        P(("gx", "gy"), None, None, None),
    )
    return jax.shard_map(
        per_device,
        mesh=mesh,
        in_specs=placed,
        out_specs=(P(None, "gx", "gy"), P(), P()),
        check_vma=False,
    )
```
